32 devices in a mesh: rep: 2 (over y), span: 2 (over core), seq: 4 (over z), tp: 2 (over x).
Axes of the slice: x: 2, y: 2, z: 4, core: 2. Of those that a mesh axis runs over, the one named last changes fastest.
Arguments:
- queries: bfloat16 [8, 512, 24, 128], P(('rep', 'span'), 'seq', 'tp'), parts along dimension 0, may hold values from -110 to 110
- key_states: bfloat16 [8, 512, 4, 128], P(('rep', 'span'), 'seq', 'tp'), parts along dimension 0, may hold values from -11 to 11
- value_states: bfloat16 [8, 512, 4, 128], P(('rep', 'span'), 'seq', 'tp'), parts along dimension 0, may hold values from -6 to 6
- out_weight: bfloat16 [3072, 6144], P('tp', 'seq'), may hold values from -0.109375 to 0.109375
- noise_table: float32 [64, 6144], P(None, 'tp'), may hold values from 0.5 to 2
- plan: int32 [8], P('rep'), parts along dimension 0, may hold values from 0 to 63
Outputs:
- branch_out: bfloat16 [8, 512, 6144], P(('rep', 'span'), 'seq', 'tp'), parts along dimension 0
The draws below stay inside these ranges and needn't reach their ends.
There are 2 independent parts, one for each index of `rep`. The reference program is written for one: setup_inputs(seed, part) draws one part's arguments, and reference() takes and returns one part's arrays. A program takes and returns all parts, laid end to end along the dimension named above; an argument that names none is the same for every part. Nothing has to cross between parts.
All inputs are finite; a program needn't handle non-finite values.
Results may differ from the reference program's by a relative error of at most 0.014.
Values may be sent and summed in bfloat16 or wider, within the bound.
No kernel may reach another device: no remote copies, remote signals or barrier semaphores. Data moves between devices by JAX's collectives and lax.ppermute only.
A program may use at most 128 MiB of HBM per device.

```python
import jax
import jax.numpy as jnp
from jax import lax

D = 6144
QH = 24
KVH = 4
HD = 128
STEPS = 64
SPANS = 4
CTOK = 512


def draw_together(key):
    base = jax.random.fold_in(key, 11)
    first, second = jax.random.split(base, 2)
    query_all = 1.6 * jax.random.truncated_normal(first, -6.0, 6.0, (SPANS, CTOK, QH, HD), jnp.float32)
    key_all = 1.6 * jax.random.truncated_normal(second, -6.0, 6.0, (SPANS, CTOK, KVH, HD), jnp.float32)
    return (query_all, key_all)


def draw_queries(key, part):
    return draw_together(key)[0].astype(jnp.bfloat16)


def draw_key_states(key, part):
    return draw_together(key)[1].astype(jnp.bfloat16)


def place_ends(drawn, own_key, least, top_value):
    place = [jax.random.randint(jax.random.fold_in(own_key, axis), (), 0, length) for axis, length in enumerate(drawn.shape)]
    widest = drawn.shape.index(max(drawn.shape))
    next_to = place[:widest] + [(place[widest] + 1) % drawn.shape[widest]] + place[widest + 1:]
    return drawn.at[tuple(place)].set(least).at[tuple(next_to)].set(top_value)


def block_scale(rng, dims, cuts, low, top_value):
    factor_of, own = 1.0, jax.random.fold_in(rng, 6)
    for axis_at, blocks in cuts:
        steps = jnp.exp(jax.random.uniform(jax.random.fold_in(own, axis_at), (blocks,), jnp.float32, low / len(cuts), top_value / len(cuts)))
        factor_of = factor_of * jnp.repeat(steps, dims[axis_at] // blocks).reshape([-1 if axis == axis_at else 1 for axis in range(len(dims))])
    return factor_of


def bell_draw(stream_key, extent, width, reach, cuts=(), kind=jnp.bfloat16):
    values = width * jax.random.normal(stream_key, extent, jnp.float32)
    if cuts:
        values = values * block_scale(stream_key, extent, cuts, -0.22, 0.18)
    return jnp.clip(values, -reach, reach).astype(kind)


def setup_inputs(seed: int = 0, part: int = 0) -> dict:
    arg_keys = jax.random.split(jax.random.key(seed), 7)
    part_splits = jax.random.split(jax.random.fold_in(arg_keys[6], part), 7)
    return {
        "queries": draw_queries(jax.random.fold_in(jax.random.fold_in(arg_keys[6], part), 71), part),
        "key_states": draw_key_states(jax.random.fold_in(jax.random.fold_in(arg_keys[6], part), 71), part),
        "value_states": bell_draw(part_splits[2], (SPANS, CTOK, KVH, HD), 1.0, 6.0, ((0, 2), (1, 4), (2, 2))),
        "out_weight": bell_draw(arg_keys[3], (QH * HD, D), (QH * HD) ** -0.5, 0.109375, ((0, 2), (1, 4))),
        "noise_table": jnp.clip(0.5 + 1.5 * jax.random.uniform(arg_keys[4], (STEPS, D), jnp.float32) ** block_scale(arg_keys[4], (STEPS, D), ((1, 2),), -0.2, 0.2), 0.5, 2.0),
        "plan": place_ends(jax.random.randint(part_splits[5], (SPANS,), 0, STEPS), jax.random.fold_in(part_splits[5], 1), 0, STEPS - 1).astype(jnp.int32),
    }


def reference(queries, key_states, value_states, out_weight, noise_table, plan):
    per_kv = QH // KVH
    factor = HD ** -0.5
    pieces = []
    for span in range(SPANS):
        key_all = key_states[:span + 1].reshape((span + 1) * CTOK, KVH, HD)
        value_all = value_states[:span + 1].reshape((span + 1) * CTOK, KVH, HD)

        def head_attend(head, span=span, key_all=key_all, value_all=value_all):
            owner = (head // per_kv).astype(jnp.int32)
            query_rows = lax.dynamic_index_in_dim(queries[span], head, 1, keepdims=False)
            key_rows = lax.dynamic_index_in_dim(key_all, owner, 1, keepdims=False)
            value_rows = lax.dynamic_index_in_dim(value_all, owner, 1, keepdims=False)
            scores = jnp.dot(query_rows, key_rows.T, preferred_element_type=jnp.float32) * factor
            highest = jnp.max(scores, axis=1, keepdims=True)
            weights = jnp.exp(scores - highest)
            totals = jnp.sum(weights, axis=1, keepdims=True)
            mixed = jnp.dot(weights.astype(jnp.bfloat16), value_rows, preferred_element_type=jnp.float32)
            return mixed / totals

        heads_out = lax.map(head_attend, jnp.arange(QH, dtype=jnp.int32))
        pieces.append(jnp.transpose(heads_out, (1, 0, 2)).reshape(CTOK, QH * HD).astype(jnp.bfloat16))
    attn = jnp.stack(pieces)
    projected = jnp.dot(attn.reshape(SPANS * CTOK, QH * HD), out_weight, preferred_element_type=jnp.float32).reshape(SPANS, CTOK, D)
    picks = (plan[:, None] == jnp.arange(STEPS, dtype=jnp.int32)[None, :]).astype(jnp.float32)
    gates = jnp.dot(picks, noise_table, precision=lax.Precision.HIGHEST)
    return (projected * gates[:, None, :]).astype(jnp.bfloat16)
```

```python
import functools
import math

import jax
import jax.numpy as jnp
from jax import lax
from jax.experimental import pallas as pl
from jax.experimental.pallas import tpu as pltpu
from jax.sharding import PartitionSpec as P

CHUNKS = 2
VMEM_SPEC = pl.BlockSpec(memory_space=pltpu.VMEM)
SMEM_SPEC = pl.BlockSpec(memory_space=pltpu.SMEM)


def tile_plan(n, m):
    owner = [s * m // n for s in range(n)]
    slot_of, tile_of = [], []
    for z in range(n):
        slots = {}
        for e in range(m):
            o = (owner[z] + e) % m
            mine = sorted((s for s in range(n) if owner[s] == o), key=lambda s: (abs(s - z), s))
            for g, s in enumerate(mine):
                slots[s] = (g, e)
        slot_of.append(slots)
        tile_of.append({q: s for s, q in slots.items()})
    hops = []
    for k in range(1, n):
        wanted = {}
        for z in range(n):
            for s in (z - k, z + k):
                if 0 <= s < n:
                    src = z - 1 if s < z else z + 1
                    wanted.setdefault(slot_of[z][s], []).append((src, z, slot_of[src][s]))
        for q in sorted(wanted):
            rest = wanted[q]
            while rest:
                used, now, later = set(), [], []
                for item in rest:
                    (later if item[0] in used else now).append(item)
                    used.add(item[0])
                hops.append((k, q, now))
                rest = later
    return owner, tile_of, hops


def among(index, members):
    hit = index == members[0]
    for other in members[1:]:
        hit = hit | (index == other)
    return hit


def attend_kernel(n, cores, scalars, q_ref, *refs):
    own, rest = refs[:n], refs[n : n * cores]
    o_ref, m_ref, l_ref, acc_ref = refs[n * cores :]
    ch, heads, tok, hd = q_ref.shape
    kvl = own[0].shape[1]
    per_kv = heads // kvl
    per_core = heads // cores
    scale = hd ** (-0.5) * math.log2(math.e)
    core = scalars[0]

    def scores_of(rows, keys):
        return (
            lax.dot_general(rows, keys, (((1,), (1,)), ((), ())), preferred_element_type=jnp.float32)
            * scale
        )

    for i in range(ch):

        def group(j, carry, i=i):
            rows = q_ref[i, pl.ds(j * per_kv, per_kv)].reshape(per_kv * tok, hd)

            def side(which, pieces, spans):
                return jnp.concatenate([p[which, j, b] for b in spans for p in pieces], axis=0)

            s = scores_of(rows, side(0, own, range(i + 1)))
            m = jnp.max(s, axis=-1, keepdims=True)
            p = jnp.exp2(s - m)
            m_ref[...] = m
            l_ref[...] = jnp.sum(p, axis=-1, keepdims=True)
            acc_ref[...] = jnp.dot(
                p.astype(jnp.bfloat16), side(1, own, range(i + 1)), preferred_element_type=jnp.float32
            )
            for r in range(1, cores):

                @pl.when(core >= r)
                def _(pieces=rest[(r - 1) * n : r * n]):
                    s = scores_of(rows, side(0, pieces, range(ch)))
                    old = m_ref[...]
                    m = jnp.maximum(old, jnp.max(s, axis=-1, keepdims=True))
                    shrink = jnp.exp2(old - m)
                    p = jnp.exp2(s - m)
                    m_ref[...] = m
                    l_ref[...] = l_ref[...] * shrink + jnp.sum(p, axis=-1, keepdims=True)
                    acc_ref[...] = acc_ref[...] * shrink + jnp.dot(
                        p.astype(jnp.bfloat16),
                        side(1, pieces, range(ch)),
                        preferred_element_type=jnp.float32,
                    )

            out = (acc_ref[...] / l_ref[...]).astype(jnp.bfloat16)
            for g in range(per_kv):
                head = j * per_kv + g
                block = lax.rem(head // per_core - core + cores, cores)
                at = block * per_core + lax.rem(head, per_core)
                o_ref[i * tok : (i + 1) * tok, pl.ds(pl.multiple_of(at * hd, hd), hd)] = out[
                    g * tok : (g + 1) * tok
                ]
            return carry

        lax.fori_loop(0, kvl, group, 0)


def project_kernel(reps, cores, m, scalars, *refs):
    rows = jnp.concatenate([a[...] for a in refs[:reps]], axis=0)
    weights = refs[reps : reps + m * cores]
    outs = refs[reps + m * cores :]
    depth = weights[0].shape[0]
    for e in range(m):
        total = None
        for r in range(cores):
            part = jnp.dot(
                rows[:, r * depth : (r + 1) * depth],
                weights[e * cores + r][...],
                preferred_element_type=jnp.float32,
            )
            total = part if total is None else total + part
        for r in range(m):

            @pl.when(scalars[1 + e] == r)
            def _(total=total, out=outs[r]):
                out[...] = total.astype(out.dtype)


def finish_kernel(groups, reps, m, ch, scalars, plan_ref, table_ref, *refs):
    out_ref = refs[-1]
    rows = out_ref.shape[0]
    tok = rows // ch
    width = refs[0].shape[1]
    per_piece = m + reps - 1
    gates = [table_ref[pl.ds(plan_ref[scalars[0] * ch + i], 1), :] for i in range(ch)]
    for a in range(groups):
        for y in range(reps):
            for j in range(CHUNKS):
                at = ((a * reps + y) * CHUNKS + j) * width
                for g in range(groups):
                    for k in range(reps):
                        first = (g * CHUNKS + j) * per_piece
                        here = (scalars[1 + m + g] == a) & (scalars[1 + m + groups + k] == y)

                        @pl.when(here)
                        def _(first=first, at=at, k=k):
                            for i in range(ch):
                                part = slice(i * tok, (i + 1) * tok)
                                if k == 0:
                                    value = refs[first][part]
                                    for r in range(1, m):
                                        value = value + refs[first + r][part].astype(jnp.float32)
                                else:
                                    value = refs[first + m + k - 1][part].astype(jnp.float32)
                                value = value * gates[i][:, at : at + width]
                                out_ref[part, at : at + width] = value.astype(out_ref.dtype)


def per_device(queries, key_states, value_states, out_weight, noise_table, plan):
    ch, tok, heads, hd = queries.shape
    n, m = lax.axis_size("seq"), lax.axis_size("tp")
    reps, cores = lax.axis_size("rep"), lax.axis_size("span")
    z, t = lax.axis_index("seq"), lax.axis_index("tp")
    rep, core = lax.axis_index("rep"), lax.axis_index("span")
    kvl = key_states.shape[2]
    features = heads * hd
    owner, tile_of, hops = tile_plan(n, m)
    groups = n // m
    depth, cols = out_weight.shape[0] // cores, out_weight.shape[1] // reps
    width = cols // CHUNKS
    rows_dev = ch * tok

    def table(values, index):
        return jnp.array(values, jnp.int32)[index]

    own_owner = table(owner, z)
    rel = [lax.rem(own_owner + e - t + m, m) for e in range(m)]
    local = jnp.array(
        [[[tile_of[p][(g, (o - owner[p]) % m)] - o * groups for g in range(groups)] for o in range(m)] for p in range(n)],
        jnp.int32,
    )[z, t]
    scalars = jnp.concatenate(
        [
            jnp.stack([core] + rel).astype(jnp.int32),
            local,
            jnp.stack([lax.rem(rep + k, reps) for k in range(reps)]).astype(jnp.int32),
        ]
    )

    pair = jnp.stack([key_states, value_states]).transpose(0, 3, 1, 2, 4)
    pieces = [pair] + [
        lax.ppermute(pair, "seq", [(i, (i + d) % n) for i in range(n)]) for d in range(1, n)
    ]
    earlier = [
        lax.ppermute(p, "span", [(i, i + r) for i in range(cores - r)])
        for r in range(1, cores)
        for p in pieces
    ]

    def block(r, j):
        return lax.dynamic_slice(
            out_weight,
            (lax.rem(core + r, cores) * depth, rep * cols + j * width),
            (depth, width),
        )

    start = (0, 0)
    held = [{start: block(0, j)} for j in range(CHUNKS)]
    for _, q, moves in hops:
        for j in range(CHUNKS):
            sources = {}
            for src, _, at in moves:
                sources.setdefault(at, []).append(src)
            sources = list(sources.items())
            sent = held[j][sources[0][0]]
            for at, who in sources[1:]:
                sent = jnp.where(among(z, who), held[j][at], sent)
            got = lax.ppermute(sent, "seq", [(src, dst) for src, dst, _ in moves])
            if q in held[j]:
                got = jnp.where(among(z, [dst for _, dst, _ in moves]), got, held[j][q])
            held[j][q] = got

    def full(q, j):
        if q == start:
            return [block(r, j) for r in range(cores)]
        return [held[j][q]] + [
            lax.ppermute(held[j][q], "span", [((i + r) % cores, i) for i in range(cores)])
            for r in range(1, cores)
        ]

    per_kv = heads // kvl
    attn = pl.pallas_call(
        functools.partial(attend_kernel, n, cores),
        out_shape=jax.ShapeDtypeStruct((rows_dev, features), jnp.bfloat16),
        in_specs=[SMEM_SPEC] + [VMEM_SPEC] * (1 + n * cores),
        out_specs=VMEM_SPEC,
        scratch_shapes=[
            pltpu.VMEM((per_kv * tok, 1), jnp.float32),
            pltpu.VMEM((per_kv * tok, 1), jnp.float32),
            pltpu.VMEM((per_kv * tok, hd), jnp.float32),
        ],
        cost_estimate=pl.CostEstimate(
            flops=4 * rows_dev * features * n * tok * ch * cores,
            bytes_accessed=4 * rows_dev * features,
            transcendentals=rows_dev * heads * n * tok * ch * cores,
        ),
        name="attend",
    )(scalars, queries.transpose(0, 2, 1, 3), *pieces, *earlier)
    token_rows = [attn] + [
        lax.ppermute(attn, "rep", [((i + k) % reps, i) for i in range(reps)]) for k in range(1, reps)
    ]

    final = []
    for g in range(groups):
        for j in range(CHUNKS):
            weights = [w for e in range(m) for w in full((g, e), j)]
            parts = pl.pallas_call(
                functools.partial(project_kernel, reps, cores, m),
                out_shape=[
                    jax.ShapeDtypeStruct((reps * rows_dev, width), jnp.float32 if r == 0 else jnp.bfloat16)
                    for r in range(m)
                ],
                in_specs=[SMEM_SPEC] + [VMEM_SPEC] * (reps + m * cores),
                out_specs=[VMEM_SPEC] * m,
                cost_estimate=pl.CostEstimate(
                    flops=2 * reps * rows_dev * features * width * m,
                    bytes_accessed=2 * (reps * rows_dev * features + m * features * width),
                    transcendentals=0,
                ),
                name="project",
            )(scalars, *token_rows, *weights)
            got = [parts[0]] + [
                lax.ppermute(parts[r], "tp", [(i, (i + r) % m) for i in range(m)]) for r in range(1, m)
            ]
            final += [p[:rows_dev] for p in got]
            for k in range(1, reps):
                part = slice(k * rows_dev, (k + 1) * rows_dev)
                summed = got[0][part]
                for p in got[1:]:
                    summed = summed + p[part].astype(jnp.float32)
                final.append(
                    lax.ppermute(
                        summed.astype(jnp.bfloat16), "rep", [(i, (i + k) % reps) for i in range(reps)]
                    )
                )
    scalars = scalars.at[1 + m + groups :].set(
        jnp.stack([lax.rem(rep - k + reps, reps) for k in range(reps)]).astype(jnp.int32)
    )
    out = pl.pallas_call(
        functools.partial(finish_kernel, groups, reps, m, ch),
        out_shape=jax.ShapeDtypeStruct((rows_dev, noise_table.shape[1]), jnp.bfloat16),
        in_specs=[SMEM_SPEC, SMEM_SPEC, VMEM_SPEC] + [VMEM_SPEC] * len(final),
        out_specs=VMEM_SPEC,
        name="finish",
    )(scalars, plan, noise_table, *final)
    return out.reshape(ch, tok, noise_table.shape[1])


def solution(mesh):
    placed = (
        P(("rep", "span"), "seq", "tp", None),
        P(("rep", "span"), "seq", "tp", None),
        P(("rep", "span"), "seq", "tp", None),
        P("tp", "seq"),
        P(None, "tp"),
        P("rep"),
    )
    return jax.shard_map(
        per_device,
        mesh=mesh,
        in_specs=placed,
        out_specs=P(("rep", "span"), "seq", "tp"),
        check_vma=False,
    )
```

```python
import functools
import math

import jax
import jax.numpy as jnp
from jax import lax
from jax.experimental import pallas as pl
from jax.experimental.pallas import tpu as pltpu
from jax.sharding import PartitionSpec as P


LANES = 128
ANY_SPEC = pl.BlockSpec(memory_space=pl.ANY)
VMEM_SPEC = pl.BlockSpec(memory_space=pltpu.VMEM)
SMEM_SPEC = pl.BlockSpec(memory_space=pltpu.SMEM)


def tile_plan(n, m):
    owner = [s * m // n for s in range(n)]
    slot_of, tile_of = [], []
    for z in range(n):
        slots = {}
        for e in range(m):
            o = (owner[z] + e) % m
            mine = sorted((s for s in range(n) if owner[s] == o), key=lambda s: (abs(s - z), s))
            for g, s in enumerate(mine):
                slots[s] = (g, e)
        slot_of.append(slots)
        tile_of.append({q: s for s, q in slots.items()})
    hops = []
    for k in range(1, n):
        wanted = {}
        for z in range(n):
            for s in (z - k, z + k):
                if 0 <= s < n:
                    src = z - 1 if s < z else z + 1
                    wanted.setdefault(slot_of[z][s], []).append((src, z, slot_of[src][s]))
        for q in sorted(wanted):
            rest = wanted[q]
            while rest:
                used, now, later = set(), [], []
                for item in rest:
                    (later if item[0] in used else now).append(item)
                    used.add(item[0])
                hops.append((k, q, now))
                rest = later
    return owner, tile_of, hops


def among(index, members):
    hit = index == members[0]
    for other in members[1:]:
        hit = hit | (index == other)
    return hit


def attend_kernel(n, cores, scalars, q_ref, *refs):
    own, rest = refs[0], refs[1:cores]
    o_ref, m_ref, l_ref, acc_ref = refs[cores:]
    ch, heads, tok, hd = q_ref.shape
    kvl = own.shape[2]
    per_kv = heads // kvl
    per_core = heads // cores
    scale = hd ** (-0.5) * math.log2(math.e)
    core = scalars[0]

    def scores_of(rows, keys):
        return (
            lax.dot_general(rows, keys, (((1,), (1,)), ((), ())), preferred_element_type=jnp.float32)
            * scale
        )

    for i in range(ch):

        def group(j, carry, i=i):
            rows = q_ref[i, pl.ds(j * per_kv, per_kv)].reshape(per_kv * tok, hd)

            def side(which, pieces, spans):
                return jnp.concatenate(
                    [pieces[p, which, j, b] for b in spans for p in range(n)], axis=0
                )

            s = scores_of(rows, side(0, own, range(i + 1)))
            m = jnp.max(s, axis=-1, keepdims=True)
            p = jnp.exp2(s - m)
            m_ref[...] = m
            l_ref[...] = jnp.sum(p, axis=-1, keepdims=True)
            acc_ref[...] = jnp.dot(
                p.astype(jnp.bfloat16), side(1, own, range(i + 1)), preferred_element_type=jnp.float32
            )
            for r in range(1, cores):

                @pl.when(core >= r)
                def _(pieces=rest[r - 1]):
                    s = scores_of(rows, side(0, pieces, range(ch)))
                    old = m_ref[...]
                    m = jnp.maximum(old, jnp.max(s, axis=-1, keepdims=True))
                    shrink = jnp.exp2(old - m)
                    p = jnp.exp2(s - m)
                    m_ref[...] = m
                    l_ref[...] = l_ref[...] * shrink + jnp.sum(p, axis=-1, keepdims=True)
                    acc_ref[...] = acc_ref[...] * shrink + jnp.dot(
                        p.astype(jnp.bfloat16),
                        side(1, pieces, range(ch)),
                        preferred_element_type=jnp.float32,
                    )

            out = (acc_ref[...] / l_ref[...]).astype(jnp.bfloat16)
            for g in range(per_kv):
                head = j * per_kv + g
                block = lax.rem(head // per_core - core + cores, cores)
                at = block * per_core + lax.rem(head, per_core)
                o_ref[i * tok : (i + 1) * tok, pl.ds(pl.multiple_of(at * hd, hd), hd)] = out[
                    g * tok : (g + 1) * tok
                ]
            return carry

        lax.fori_loop(0, kvl, group, 0)


def project_kernel(reps, m, cores, choices, pick_at, scalars, *refs):
    rows = refs[:reps]
    given = refs[reps : reps + sum(choices) * cores]
    outs = refs[reps + len(given) : -4]
    rows_buf, weights_buf, rows_sem, weights_sem = refs[-4:]
    count = rows[0].shape[0]
    depth = given[0].shape[0]
    loads = []
    for k in range(reps):
        load = pltpu.make_async_copy(
            rows[k], rows_buf.at[k * count : (k + 1) * count], rows_sem.at[k]
        )
        load.start()
        loads.append(load)
    waits = [[None] * cores for _ in range(m)]
    first = 0
    for e in range(m):
        for v in range(choices[e]):
            for r in range(cores):
                load = pltpu.make_async_copy(
                    given[first + r],
                    weights_buf.at[e, r * depth : (r + 1) * depth],
                    weights_sem.at[e, r],
                )
                waits[e][r] = load
                if choices[e] == 1:
                    load.start()
                else:
                    pl.when(scalars[pick_at[e]] == v)(load.start)
            first += cores
    for load in loads:
        load.wait()
    for e in range(m):
        for load in waits[e]:
            load.wait()
        total = jnp.dot(rows_buf[...], weights_buf[e], preferred_element_type=jnp.float32)
        for r in range(m):

            @pl.when(scalars[1 + e] == r)
            def _(total=total, r=r):
                for k in range(reps):
                    out = outs[r * reps + k]
                    out[...] = total[k * count : (k + 1) * count].astype(out.dtype)


def finish_kernel(reps, m, ch, cols, offset, group_at, block_at, scalars, gates_ref, *refs):
    pieces = refs[: reps * m]
    out_ref, buf, sem = refs[-3:]
    width = buf.shape[2]
    tok = buf.shape[1] // ch
    stores = []
    for k in range(reps):
        at = (scalars[group_at] * reps + scalars[block_at + k]) * cols + offset
        at = pl.multiple_of(at, LANES)
        for i in range(ch):
            part = slice(i * tok, (i + 1) * tok)
            value = pieces[k * m][part].astype(jnp.float32)
            for r in range(1, m):
                value = value + pieces[k * m + r][part].astype(jnp.float32)
            value = value * gates_ref[i : i + 1, pl.ds(at, width)]
            buf[k, part] = value.astype(buf.dtype)
        store = pltpu.make_async_copy(buf.at[k], out_ref.at[:, pl.ds(at, width)], sem.at[k])
        store.start()
        stores.append(store)
    for store in stores:
        store.wait()


def column_chunks(cols):
    if cols % LANES or cols < 2 * LANES:
        return [(0, cols)]
    last = max(LANES, cols // 3 // LANES * LANES)
    return [(0, cols - last), (cols - last, last)]


def per_device(queries, key_states, value_states, out_weight, noise_table, plan):
    ch, tok, heads, hd = queries.shape
    n, m = lax.axis_size("seq"), lax.axis_size("tp")
    reps, cores = lax.axis_size("rep"), lax.axis_size("span")
    z, t = lax.axis_index("seq"), lax.axis_index("tp")
    rep, core = lax.axis_index("rep"), lax.axis_index("span")
    kvl = key_states.shape[2]
    features = heads * hd
    owner, tile_of, hops = tile_plan(n, m)
    groups = n // m
    depth, cols = out_weight.shape[0] // cores, out_weight.shape[1] // reps
    chunks = column_chunks(cols)
    rows_dev = ch * tok

    pair = jnp.stack([key_states, value_states]).transpose(0, 3, 1, 2, 4)
    pieces = [pair]
    for d in range(1, n):
        pieces.append(lax.ppermute(pair, "seq", [(i, (i + d) % n) for i in range(n)]))
    pieces = jnp.stack(pieces)
    earlier = []
    for r in range(1, cores):
        earlier.append(lax.ppermute(pieces, "span", [(i, i + r) for i in range(cores - r)]))

    def block(source, r, j):
        return lax.dynamic_slice(
            source,
            (lax.rem(core + r, cores) * depth, rep * cols + chunks[j][0]),
            (depth, chunks[j][1]),
        )

    start = (0, 0)
    held = [{start: [block(out_weight, 0, j)]} for j in range(len(chunks))]
    source_of = {start: {p: 0 for p in range(n)}}
    for _, q, moves in hops:
        version = len(held[0].get(q, []))
        for j in range(len(chunks)):
            sources = {}
            for src, _, at in moves:
                sources.setdefault((at, source_of[at][src]), []).append(src)
            sources = list(sources.items())
            (at, v), _ = sources[0]
            sent = held[j][at][v]
            for (at, v), who in sources[1:]:
                sent = jnp.where(among(z, who), held[j][at][v], sent)
            got = lax.ppermute(sent, "seq", [(src, dst) for src, dst, _ in moves])
            held[j].setdefault(q, []).append(got)
        for _, dst, _ in moves:
            source_of.setdefault(q, {})[dst] = version
    slots = [(g, e) for g in range(groups) for e in range(m)]

    own_owner = jnp.array(owner, jnp.int32)[z]
    rel = [lax.rem(own_owner + e - t + m, m) for e in range(m)]
    local = jnp.array(
        [
            [
                [tile_of[p][(g, (o - owner[p]) % m)] - o * groups for g in range(groups)]
                for o in range(m)
            ]
            for p in range(n)
        ],
        jnp.int32,
    )[z, t]
    picks = jnp.array([[source_of[q][p] for q in slots] for p in range(n)], jnp.int32)[z]
    blocks = [lax.rem(rep - k + reps, reps) for k in range(reps)]
    scalars = jnp.concatenate(
        [
            jnp.stack([core] + rel).astype(jnp.int32),
            local,
            jnp.stack(blocks).astype(jnp.int32),
            picks,
        ]
    )
    group_at = 1 + m
    block_at = group_at + groups
    pick_at = block_at + reps
    gates = jnp.concatenate(
        [lax.dynamic_slice_in_dim(noise_table, plan[core * ch + i], 1, 0) for i in range(ch)]
    )

    def full(q, v, j):
        first = held[j][q][v]
        if q == start:
            late = lax.optimization_barrier((out_weight, pieces))[0]
            return [first] + [block(late, r, j) for r in range(1, cores)]
        whole = [first]
        for r in range(1, cores):
            whole.append(lax.ppermute(first, "span", [((i + r) % cores, i) for i in range(cores)]))
        return whole

    per_kv = heads // kvl
    attn = pl.pallas_call(
        functools.partial(attend_kernel, n, cores),
        out_shape=jax.ShapeDtypeStruct((rows_dev, features), jnp.bfloat16),
        in_specs=[SMEM_SPEC] + [VMEM_SPEC] * (1 + cores),
        out_specs=VMEM_SPEC,
        scratch_shapes=[
            pltpu.VMEM((per_kv * tok, 1), jnp.float32),
            pltpu.VMEM((per_kv * tok, 1), jnp.float32),
            pltpu.VMEM((per_kv * tok, hd), jnp.float32),
        ],
        cost_estimate=pl.CostEstimate(
            flops=4 * rows_dev * features * n * tok * ch * cores,
            bytes_accessed=4 * rows_dev * features,
            transcendentals=rows_dev * heads * n * tok * ch * cores,
        ),
        name="attend",
    )(scalars, queries.transpose(0, 2, 1, 3), pieces, *earlier)
    token_rows = [attn]
    for k in range(1, reps):
        token_rows.append(
            lax.ppermute(attn, "rep", [((i + k) % reps, i) for i in range(reps)])
        )

    out = None
    out_cols = noise_table.shape[1]
    aligned = cols % LANES == 0
    for g in range(groups):
        for j, (offset, width) in enumerate(chunks):
            mine = [(g, e) for e in range(m)]
            choices = [len(held[j][q]) for q in mine]
            weights = [
                w for q in mine for v in range(len(held[j][q])) for w in full(q, v, j)
            ]
            parts = pl.pallas_call(
                functools.partial(
                    project_kernel,
                    reps,
                    m,
                    cores,
                    choices,
                    [pick_at + slots.index(q) for q in mine],
                ),
                out_shape=[
                    jax.ShapeDtypeStruct((rows_dev, width), jnp.bfloat16 if r or k else jnp.float32)
                    for r in range(m)
                    for k in range(reps)
                ],
                in_specs=[SMEM_SPEC] + [ANY_SPEC] * (reps + len(weights)),
                out_specs=[VMEM_SPEC] * (m * reps),
                scratch_shapes=[
                    pltpu.VMEM((reps * rows_dev, features), jnp.bfloat16),
                    pltpu.VMEM((m, features, width), jnp.bfloat16),
                    pltpu.SemaphoreType.DMA((reps,)),
                    pltpu.SemaphoreType.DMA((m, cores)),
                ],
                cost_estimate=pl.CostEstimate(
                    flops=2 * reps * rows_dev * features * width * m,
                    bytes_accessed=2 * (reps * rows_dev * features + m * features * width),
                    transcendentals=0,
                ),
                name="project",
            )(scalars, *token_rows, *weights)
            arrived = {(0, 0): parts[0]}
            order = [(r, k) for r in range(m) for k in range(reps) if r or k]
            for r, k in sorted(order, key=lambda rk: -(rk[0] > 0) - (rk[1] > 0)):
                moves = [
                    (y * m + x, (y + k) % reps * m + (x + r) % m)
                    for y in range(reps)
                    for x in range(m)
                ]
                arrived[r, k] = lax.ppermute(parts[r * reps + k], ("rep", "tp"), moves)
            terms = [arrived[r, k] for k in range(reps) for r in range(m)]
            if aligned:
                before = [] if out is None else [out]
                out = pl.pallas_call(
                    functools.partial(
                        finish_kernel, reps, m, ch, cols, offset, group_at + g, block_at
                    ),
                    out_shape=jax.ShapeDtypeStruct((rows_dev, out_cols), jnp.bfloat16),
                    in_specs=[SMEM_SPEC]
                    + [VMEM_SPEC] * (1 + len(terms))
                    + [ANY_SPEC] * len(before),
                    out_specs=ANY_SPEC,
                    scratch_shapes=[
                        pltpu.VMEM((reps, rows_dev, width), jnp.bfloat16),
                        pltpu.SemaphoreType.DMA((reps,)),
                    ],
                    input_output_aliases={2 + len(terms): 0} if before else {},
                    name="finish",
                )(scalars, gates, *terms, *before)
                continue
            if out is None:
                out = jnp.zeros((rows_dev, out_cols), jnp.bfloat16)
            for k in range(reps):
                at = (local[g] * reps + blocks[k]) * cols + offset
                value = sum(x.astype(jnp.float32) for x in terms[k * m : (k + 1) * m])
                gate = lax.dynamic_slice_in_dim(gates, at, width, 1)
                value = value.reshape(ch, tok, width) * gate[:, None]
                out = lax.dynamic_update_slice(
                    out, value.reshape(rows_dev, width).astype(out.dtype), (0, at)
                )
    return out.reshape(ch, tok, out_cols)


def solution(mesh):
    placed = (
        P(("rep", "span"), "seq", "tp", None),
        P(("rep", "span"), "seq", "tp", None),
        P(("rep", "span"), "seq", "tp", None),
        P("tp", "seq"),
        P(None, "tp"),
        P("rep"),
    )

    return jax.shard_map(
        per_device,
        mesh=mesh,
        in_specs=placed,
        out_specs=P(("rep", "span"), "seq", "tp"),
        check_vma=False,
    )
```
